256 devices in a mesh: shard: 16 (over x, z_hi, core), rep: 16 (over y, z_lo).
Axes of the slice: x: 4, y: 4, z: 8 (z_hi: 2, z_lo: 4; z = z_hi * 4 + z_lo), core: 2. Of those that a mesh axis runs over, the one named last changes fastest.
Arguments:
- grads: bfloat16 [16, 16, 2097152], P('shard', 'rep'), may hold values from -5000 to 5000
- momentum_codes: int32 [2097152], P(('shard', 'rep')), may hold values from -127 to 127
- variance_codes: int32 [2097152], P(('shard', 'rep')), may hold values from 16 to 255
- momentum_scale: float32 [1280], P(('shard', 'rep')), may hold values from 0.5 to 4, as said below
- variance_scale: float32 [1280], P(('shard', 'rep')), may hold values from 1 to 4, as said below
- master: float32 [2097152], P(('shard', 'rep')), may hold values from -2.5 to 2.5
- step: int32 [1], replicated, may hold values from 1 to 19
Outputs:
- new_master: float32 [2097152], P(('shard', 'rep'))
- weights: bfloat16 [2097152], P('shard')
- update: float32 [2097152], P(('shard', 'rep'))
- momentum_norm: float32 [2097152], P(('shard', 'rep'))
- variance_norm: float32 [2097152], P(('shard', 'rep'))
- momentum_absmax: float32 [1280], P(('shard', 'rep'))
- variance_absmax: float32 [1280], P(('shard', 'rep'))
The draws below stay inside these ranges and needn't reach their ends.
Inputs may be any that keep to these rules, and one draw needn't show every extreme that they name: `momentum_scale`: A block touched by two neighbouring devices has the same value in both devices' slots. `variance_scale`: A block touched by two neighbouring devices has the same value in both devices' slots.
All inputs are finite; a program needn't handle non-finite values.
Results may differ from the reference program's by a relative error of at most 0.0004.
Values may be sent and summed in bfloat16 or wider, within the bound.
A program may use at most 64 MiB of HBM per device.

```python
import math
import jax
import jax.numpy as jnp
from jax import lax

BLOCK = 2048
FULL_BLOCKS = 4
OWN = 8192
SLOTS = 5
PARAMS = 2097152
N_SHARD = 16
N_REP = 16
DEVICES = 256


def slot_blocks():
    owner = jnp.arange(DEVICES, dtype=jnp.int32)[:, None]
    slot = jnp.arange(SLOTS, dtype=jnp.int32)[None, :]
    return (owner * FULL_BLOCKS + slot).reshape(-1).astype(jnp.int32)


def draw_scale(key, low, high):
    nblocks = PARAMS // BLOCK + 1
    values = jnp.exp(jax.random.uniform(key, (nblocks,), jnp.float32, math.log(low), math.log(high)))
    return values[slot_blocks()]


def draw_momentum_scale(key, part):
    return draw_scale(jax.random.fold_in(key, 11), 0.5, 4.0)


def draw_variance_scale(key, part):
    return draw_scale(jax.random.fold_in(key, 23), 1.0, 4.0)


def plant_codes(key, low, high, peak, upper, signed):
    nblocks = PARAMS // BLOCK + 1
    half_len = BLOCK // 2
    key_base, key_place, key_sign = jax.random.split(key, 3)
    base = jax.random.randint(key_base, (PARAMS,), low, high, dtype=jnp.int32)
    entry = jnp.arange(PARAMS, dtype=jnp.int32)
    block = (entry + half_len) // BLOCK
    within = (entry + half_len) % BLOCK
    place = jax.random.randint(key_place, (nblocks,), 0, half_len, dtype=jnp.int32)
    if upper:
        place = place + half_len
    chosen = within == place[block]
    if signed:
        signs = jax.random.randint(key_sign, (nblocks,), 0, 2, dtype=jnp.int32) * 2 - 1
        signs = signs.at[0].set(1).at[1].set(-1)
        planted = peak * signs[block]
    else:
        planted = jnp.full((PARAMS,), peak, jnp.int32)
    return jnp.where(chosen, planted, base).astype(jnp.int32)


def draw_momentum_codes(key, part):
    return plant_codes(jax.random.fold_in(key, 41), -63, 64, 127, True, True)


def draw_variance_codes(key, part):
    return plant_codes(jax.random.fold_in(key, 43), 16, 129, 255, False, False)


def draw_grads(key, part):
    keys = jax.random.split(jax.random.fold_in(key, 37), 9)
    nblocks = PARAMS // BLOCK
    position = jnp.arange(PARAMS, dtype=jnp.float32) / float(PARAMS)
    roughness = jnp.repeat(jnp.exp(jax.random.uniform(keys[0], (nblocks,), jnp.float32, 0.0, math.log(10.0))), BLOCK)
    device_scale = jnp.exp(jax.random.uniform(keys[1], (N_SHARD, N_REP, 1), jnp.float32, 0.0, math.log(3.0)))
    noise = jnp.clip(jax.random.normal(keys[2], (N_SHARD, N_REP, PARAMS), jnp.float32), -4.0, 4.0)
    perm_a = jax.random.permutation(keys[3], N_SHARD).astype(jnp.int32)
    perm_b = jax.random.permutation(keys[4], N_REP).astype(jnp.int32)
    partner = perm_a[:, None] * N_REP + perm_b[None, :]
    owner = jnp.arange(PARAMS, dtype=jnp.int32) // OWN
    heavy = (owner[None, None, :] == partner[:, :, None]).astype(jnp.float32)
    spike = 1.0 + 11.0 * heavy
    trend = jnp.power(3.0, position) * roughness
    quarter = BLOCK // 4
    odd_step = 2 * jax.random.randint(keys[6], (nblocks,), 0, max(quarter // 2, 1), dtype=jnp.int32) + 1
    region = jax.random.randint(keys[7], (nblocks,), 0, 2, dtype=jnp.int32)
    offset = quarter + region * 2 * quarter + odd_step
    sign_flip = (jax.random.randint(keys[8], (nblocks,), 0, 2, dtype=jnp.int32) * 2 - 1).astype(jnp.float32)
    entry = jnp.arange(PARAMS, dtype=jnp.int32)
    group_of = entry // BLOCK
    within = entry % BLOCK
    planted = (within == offset[group_of]).astype(jnp.float32) * sign_flip[group_of]
    spread_sq = 3.64 * float(DEVICES + 143)
    values = noise * device_scale * spike * trend
    height = math.sqrt(float(BLOCK) * spread_sq) / float(DEVICES)
    values = values + (height * planted * trend)[None, None, :]
    return values.astype(jnp.bfloat16)


def level_of(stream_key, extent, pieces, low, top_value):
    def one(axis_at, blocks):
        heights = jax.random.uniform(jax.random.fold_in(jax.random.fold_in(stream_key, 6), axis_at), (blocks,), jnp.float32, low / len(pieces), top_value / len(pieces))
        return jnp.repeat(jnp.exp(heights), extent[axis_at] // blocks).reshape((-1,) + (1,) * (len(extent) - axis_at - 1))

    gain = one(*pieces[0])
    for cut in pieces[1:]:
        gain = gain * one(*cut)
    return gain


def gaussian(key, shape, deviation, reach, cuts=(), kind=jnp.bfloat16):
    array = deviation * jax.random.normal(key, shape, jnp.float32)
    if cuts:
        array = array * level_of(key, shape, cuts, -0.22, 0.18)
    return jnp.clip(array, -reach, reach).astype(kind)


def setup_inputs(seed: int = 0) -> dict:
    key_of = jax.random.split(jax.random.key(seed), 8)
    grads = draw_grads(jax.random.fold_in(key_of[7], 71), 0)
    momentum_codes = draw_momentum_codes(jax.random.fold_in(key_of[7], 71), 0)
    variance_codes = draw_variance_codes(jax.random.fold_in(key_of[7], 71), 0)
    momentum_scale = draw_momentum_scale(jax.random.fold_in(key_of[7], 71), 0)
    variance_scale = draw_variance_scale(jax.random.fold_in(key_of[7], 71), 0)
    master = gaussian(key_of[5], (PARAMS,), 0.5, 2.5, ((0, 256),), jnp.float32)
    step = jax.random.randint(key_of[6], (1,), 1, 20).astype(jnp.int32)
    return {"grads": grads, "momentum_codes": momentum_codes, "variance_codes": variance_codes, "momentum_scale": momentum_scale, "variance_scale": variance_scale, "master": master, "step": step}


def slot_index():
    entry = jnp.arange(PARAMS, dtype=jnp.int32)
    owner = entry // OWN
    local = entry % OWN
    slot = (local + BLOCK // 2) // BLOCK
    return (owner * SLOTS + slot).astype(jnp.int32)

def block_of_slot():
    owner = jnp.arange(DEVICES, dtype=jnp.int32)[:, None]
    slot = jnp.arange(SLOTS, dtype=jnp.int32)[None, :]
    return (owner * FULL_BLOCKS + slot).reshape(-1).astype(jnp.int32)

def reference(grads, momentum_codes, variance_codes, momentum_scale, variance_scale, master, step):
    half = BLOCK // 2
    gsum = lax.optimization_barrier(jnp.sum(grads.astype(jnp.float32), axis=(0, 1)))
    norm_sq = jnp.sum(gsum * gsum)
    clip_factor = jnp.minimum(1.0, float(PARAMS) ** 0.5 / (jnp.sqrt(norm_sq) + 1e-06))
    scaled = gsum * clip_factor
    index = slot_index()
    m_old = momentum_codes.astype(jnp.float32) / 127.0 * momentum_scale[index]
    v_old = variance_codes.astype(jnp.float32) / 255.0 * variance_scale[index]
    momentum = 0.9 * m_old + 0.1 * scaled
    variance = 0.95 * v_old + 0.05 * scaled * scaled
    count = step[0].astype(jnp.float32)
    first_fix = 1.0 - jnp.power(jnp.float32(0.9), count)
    second_fix = 1.0 - jnp.power(jnp.float32(0.95), count)
    update = momentum / first_fix / (jnp.sqrt(variance / second_fix) + 1e-08)
    new_master = master * (1.0 - 0.0001 * 0.1) - 0.0001 * update
    weights = new_master.astype(jnp.bfloat16)
    nblocks = PARAMS // BLOCK + 1
    m_pad = jnp.pad(jnp.abs(momentum), (half, half))
    v_pad = jnp.pad(jnp.abs(variance), (half, half))
    m_block = lax.optimization_barrier(jnp.max(m_pad.reshape(nblocks, BLOCK), axis=1))
    v_block = lax.optimization_barrier(jnp.max(v_pad.reshape(nblocks, BLOCK), axis=1))
    m_elem = jnp.repeat(m_block, BLOCK)[half:half + PARAMS]
    v_elem = jnp.repeat(v_block, BLOCK)[half:half + PARAMS]
    momentum_norm = momentum / (m_elem + 1e-06)
    variance_norm = variance / (v_elem + 1e-06)
    slots = block_of_slot()
    return (new_master, weights, update, momentum_norm, variance_norm, m_block[slots], v_block[slots])
```

```python
import math

import jax
import jax.numpy as jnp
from jax import lax
from jax.experimental import pallas as pl
from jax.experimental.pallas import tpu as pltpu
from jax.sharding import PartitionSpec as P

MESH = pl.DeviceIdType.MESH
F32 = jnp.float32
BF16 = jnp.bfloat16
OWN = 8192
ROWS = 64
PIECE = 4 * OWN
CORE_RUN = 4 * PIECE
HALF = 8 * CORE_RUN
RA, RB, RC = 24, 24, 16
SLOT_ROWS = ((0, 8), (8, 24), (24, 40), (40, 56), (56, 64))


def mod(v, n):
    return lax.rem(v + 4 * n, n)


class Copies:
    def __init__(self):
        self.sent = []

    def start(self, copy):
        copy.start()
        self.sent.append(copy)

    def finish(self):
        for copy in self.sent:
            copy.wait_send()


class Ring:
    def __init__(self, out, pos, n, work, land, send, recv, peer):
        self.out, self.pos, self.n = out, pos, n
        self.work, self.land, self.send, self.recv, self.peer = work, land, send, recv, peer
        self.index = {}
        for s, h in ((1, 0), (-1, 1), (1, 1), (-1, 0)):
            for k in range(1, self.hops(s, h) + 1):
                self.index[s, h, k] = len(self.index)

    def hops(self, s, h):
        return self.n // 2 if (s == 1) == (h == 0) else self.n // 2 - 1

    def at(self, offset):
        return mod(self.pos + offset, self.n)

    def copy(self, s, h, k):
        i = self.index[s, h, k]
        return pltpu.make_async_remote_copy(
            src_ref=self.work.at[self.at(s * (self.hops(s, h) - k + 1)), h],
            dst_ref=self.land.at[i],
            send_sem=self.send.at[i],
            recv_sem=self.recv.at[i],
            device_id=self.peer(s),
            device_id_type=MESH,
        )

    def start(self, s, h, k=1):
        self.out.start(self.copy(s, h, k))

    def step(self, s, h, k):
        self.copy(s, h, k).wait_recv()
        hops = self.hops(s, h)
        if k < hops:
            dest = self.at(s * (hops - k))
            self.work[dest, h] = self.work[dest, h] + self.land[self.index[s, h, k]]
            self.start(s, h, k + 1)

    def total(self, h):
        t = self.work[self.pos, h]
        for s in (1, -1):
            t = t + self.land[self.index[s, h, self.hops(s, h)]]
        return t


def kernel(
    g_ref, mc_ref, vc_ref, ms_ref, vs_ref, ma_ref, st_ref,
    nm_ref, wt_ref, up_ref, mn_ref, vn_ref, tb_ref,
    own, par, wa, wb, wc, la, lb, lc, sa, sb, sc, la2, lb2, ta, tb2, qa, qb, qc,
    nv, nq, nv2, nq2, ex, fx, wg,
    own_sem, par_s, par_r, a_s, a_r, b_s, b_r, c_s, c_r, a2_s, a2_r, b2_s, b2_r,
    qa_s, qa_r, qb_s, qb_r, qc_s, qc_r, n_s, n_r, n2_s, n2_r, e_s, e_r, w_s, w_r,
):
    shard = lax.axis_index("shard")
    rep = lax.axis_index("rep")
    x, zh, c = shard // 4, (shard // 2) % 2, shard % 2
    y, zl = rep // 4, rep % 4
    z = zh * 4 + zl

    def dev(xx, yy, zz, cc):
        xx, yy, zz, cc = mod(xx, 4), mod(yy, 4), mod(zz, 8), mod(cc, 2)
        return (xx * 4 + (zz // 4) * 2 + cc, yy * 4 + zz % 4)

    out = Copies()

    def remote(src, dst, send, recv, device):
        return pltpu.make_async_remote_copy(
            src_ref=src, dst_ref=dst, send_sem=send, recv_sem=recv, device_id=device, device_id_type=MESH
        )

    barrier = pltpu.get_barrier_semaphore()
    near = [dev(x, y, z, c + 1)]
    for s in (1, -1):
        near += [dev(x + s, y, z, c), dev(x, y + s, z, c), dev(x, y, z + s, c)]
    for device in near:
        pl.semaphore_signal(barrier, inc=1, device_id=device, device_id_type=MESH)

    groups = (
        [(2, d, e) for d in (1, 0) for e in range(4)],
        [(d, e, 2) for d in (1, 3, 0) for e in (1, 0)],
        [(d, 1, e) for d in (1, 3, 0) for e in (1, 3, 0)],
        [(d, 0, e) for d in (1, 3, 0) for e in (1, 3, 0)],
    )

    def piece_of(rel):
        return (mod(x + rel[0], 4) * 2 + mod(zh + rel[1], 2)) * 4 + mod(y + rel[2], 4)

    def window(ref, start):
        return ref.at[:, :, pl.ds(pl.multiple_of(start, PIECE), PIECE)]

    def start_of(piece, core):
        return (piece // 4) * (2 * CORE_RUN) + core * CORE_RUN + (piece % 4) * PIECE

    def local_piece(rel):
        p = piece_of(rel)
        return pltpu.make_async_copy(window(g_ref, start_of(p, c)), window(own, p * PIECE), own_sem.at[p])

    def partner_piece(rel):
        p = piece_of(rel)
        return remote(
            window(g_ref, start_of(p, 1 - c)), window(par, p * PIECE), par_s.at[p], par_r.at[p], dev(x, y, z, c + 1)
        )

    for group in groups:
        for rel in group:
            local_piece(rel).start()
    pl.semaphore_wait(barrier, len(near))
    for group in groups:
        for rel in group:
            out.start(partner_piece(rel))

    def arrive(group):
        for rel in group:
            local_piece(rel).wait()
            partner_piece(rel).wait_recv()

    def pair(block, first, rows):
        at = pl.ds(pl.multiple_of(block * OWN + first * 128, 1024), rows * 128)
        return own[0, 0, at].reshape(rows, 128).astype(F32) + par[0, 0, at].reshape(rows, 128).astype(F32)

    def sum_a(dx, h):
        xx = mod(x + dx, 4)

        def body(j, carry):
            base = ((xx * 2 + j % 2) * 4 + (h * 2 + j // 2)) * 4
            for i in range(4):
                wa[xx, h, j * 4 + i] = pair(base + i, 0, RA)
            return carry

        lax.fori_loop(0, 4, body, 0)

    def sum_b(dy, h):
        yy = mod(y + dy, 4)

        def body(j, carry):
            base = (((h * 2 + j // 2) * 2 + j % 2) * 4 + yy) * 4
            for i in range(4):
                wb[yy, h, j * 4 + i] = pair(base + i, RA, RB)
            return carry

        lax.fori_loop(0, 4, body, 0)

    def sum_c(dz, h):
        zz = mod(z + dz, 8)

        def body(j, carry):
            base = (((h * 2 + j) * 2 + zz // 4) * 4) * 4 + zz % 4
            for i in range(4):
                wc[zz, h, j * 4 + i] = pair(base + 4 * i, RA + RB, RC)
            return carry

        lax.fori_loop(0, 2, body, 0)

    a1 = Ring(out, x, 4, wa, la, a_s, a_r, lambda s: dev(x + s, y, z, c))
    b1 = Ring(out, y, 4, wb, lb, b_s, b_r, lambda s: dev(x, y + s, z, c))
    c1 = Ring(out, z, 8, wc, lc, c_s, c_r, lambda s: dev(x, y, z + s, c))
    a2 = Ring(out, y, 4, sa, la2, a2_s, a2_r, lambda s: dev(x, y + s, z, c))
    b2 = Ring(out, x, 4, sb, lb2, b2_s, b2_r, lambda s: dev(x + s, y, z, c))

    arrive(groups[0])
    sum_a(2, 0)
    a1.start(1, 0)
    sum_a(2, 1)
    a1.start(-1, 1)
    arrive(groups[1])
    sum_b(2, 0)
    b1.start(1, 0)
    sum_b(2, 1)
    b1.start(-1, 1)
    arrive(groups[2])
    sum_c(4, 0)
    c1.start(1, 0)
    sum_c(4, 1)
    c1.start(-1, 1)
    arrive(groups[3])
    sum_c(3, 1)
    c1.start(1, 1)
    sum_c(-3, 0)
    c1.start(-1, 0)
    sum_a(1, 1)
    a1.start(1, 1)
    sum_a(-1, 0)
    a1.start(-1, 0)
    sum_b(1, 1)
    b1.start(1, 1)
    sum_b(-1, 0)
    b1.start(-1, 0)
    sum_c(3, 0)
    sum_c(-3, 1)
    sum_a(1, 0)
    sum_a(-1, 1)
    sum_b(1, 0)
    sum_b(-1, 1)
    for h in (0, 1):
        sum_c(2, h)
        sum_c(-2, h)
    for h in (0, 1):
        sum_c(1, h)
        sum_c(-1, h)
    for h in (0, 1):
        sum_a(0, h)
        sum_b(0, h)
        sum_c(0, h)

    def long_step(ring, k):
        ring.step(1, 0, k)
        ring.step(-1, 1, k)

    def short_step(ring, k):
        ring.step(1, 1, k)
        ring.step(-1, 0, k)

    def begin(ring):
        for s, h in ((1, 0), (-1, 1), (1, 1), (-1, 0)):
            ring.start(s, h)

    steps = st_ref[0]
    first_pow = jnp.ones((8, 128), F32)
    second_pow = jnp.ones((8, 128), F32)
    taken = jnp.full((8, 128), steps, jnp.int32)
    for i in range(19):
        first_pow = jnp.where(taken > i, first_pow * 0.9, first_pow)
        second_pow = jnp.where(taken > i, second_pow * 0.95, second_pow)
    first_fix = (1.0 - first_pow)[0:1]
    second_fix = (1.0 - second_pow)[0:1]

    def spread(scale_ref):
        return jnp.concatenate([jnp.full((b - a, 128), scale_ref[i], F32) for i, (a, b) in enumerate(SLOT_ROWS)], axis=0)

    long_step(c1, 1)
    long_step(a1, 1)
    short_step(c1, 1)
    long_step(b1, 1)
    long_step(c1, 2)
    short_step(c1, 2)
    short_step(a1, 1)
    long_step(a1, 2)
    for h in (0, 1):
        t = a1.total(h)
        for i in range(2):
            for j in range(2):
                sa[h * 2 + i, j] = t[i * 8 + j * 4 : i * 8 + j * 4 + 4]
    begin(a2)
    long_step(c1, 3)
    short_step(b1, 1)
    long_step(b1, 2)
    for h in (0, 1):
        t = b1.total(h)
        for i in range(2):
            for j in range(2):
                sb[h * 2 + i, j] = t[i * 8 + j * 4 : i * 8 + j * 4 + 4]
    begin(b2)
    long_step(a2, 1)
    short_step(c1, 3)
    long_step(c1, 4)
    for h in (0, 1):
        t = c1.total(h)
        for i in range(2):
            sc[h * 2 + i] = t[i * 4 : i * 4 + 4]
    plane = [(i, j) for i in range(4) for j in range(4) if i or j]

    def plane_copy(i):
        dx, dy = plane[i]
        return remote(
            sc.at[mod(x + dx, 4), mod(y + dy, 4)], qc.at[i], qc_s.at[i], qc_r.at[i], dev(x + dx, y + dy, z, c)
        )

    for i in range(len(plane)):
        out.start(plane_copy(i))
    long_step(b2, 1)
    short_step(a2, 1)
    long_step(a2, 2)
    for h in (0, 1):
        ta[h * 4 : h * 4 + 4] = a2.total(h)

    def z_copy(src, dst, send, recv, i):
        return remote(src.at[mod(z + i + 1, 8)], dst.at[i], send.at[i], recv.at[i], dev(x, y, z + i + 1, c))

    for i in range(7):
        out.start(z_copy(ta, qa, qa_s, qa_r, i))
    short_step(b2, 1)
    long_step(b2, 2)
    for h in (0, 1):
        tb2[h * 4 : h * 4 + 4] = b2.total(h)
    for i in range(7):
        out.start(z_copy(tb2, qb, qb_s, qb_r, i))

    m_base = 0.9 * (mc_ref[...].astype(F32) / 127.0 * spread(ms_ref))
    v_base = 0.95 * (vc_ref[...].astype(F32) / 255.0 * spread(vs_ref))
    kept = ma_ref[...] * (1.0 - 0.0001 * 0.1)

    gc = sc[x, y]
    for i in range(len(plane)):
        plane_copy(i).wait_recv()
        gc = gc + qc[i]
    ga = ta[z]
    for i in range(7):
        z_copy(ta, qa, qa_s, qa_r, i).wait_recv()
        ga = ga + qa[i]
    gb = tb2[z]
    for i in range(7):
        z_copy(tb2, qb, qb_s, qb_r, i).wait_recv()
        gb = gb + qb[i]
    gsum = jnp.concatenate([ga, gb, gc], axis=0)

    nv[...] = jnp.sum(gsum * gsum, axis=0, keepdims=True)
    around = [(i, j, k) for i in range(4) for j in range(4) for k in range(2) if i or j or k]

    def norm_copy(i):
        dx, dy, dc = around[i]
        return remote(nv, nq.at[i], n_s.at[i], n_r.at[i], dev(x + dx, y + dy, z, c + dc))

    for i in range(len(around)):
        out.start(norm_copy(i))
    n1 = nv[...]
    for i in range(len(around)):
        norm_copy(i).wait_recv()
        n1 = n1 + nq[i]
    nv2[...] = n1

    def norm_copy2(i):
        return remote(nv2, nq2.at[i], n2_s.at[i], n2_r.at[i], dev(x, y, z + i + 1, c))

    for i in range(7):
        out.start(norm_copy2(i))
    for i in range(7):
        norm_copy2(i).wait_recv()
        n1 = n1 + nq2[i]
    norm_sq = jnp.sum(n1, axis=1, keepdims=True)
    limit = math.sqrt(float(OWN * 256))
    clip = jnp.minimum(1.0, limit / (jnp.sqrt(norm_sq) + 1e-06))

    scaled = gsum * clip
    momentum = m_base + 0.1 * scaled
    variance = v_base + 0.05 * scaled * scaled
    update = momentum / first_fix / (jnp.sqrt(variance / second_fix) + 1e-08)
    fresh = kept - 0.0001 * update
    wg[rep] = fresh.astype(BF16)

    def along_z(i):
        zz = mod(zl + i, 4)
        return remote(wg.at[rep], wg.at[rep], w_s.at[i - 1], w_r.at[rep], dev(x, y, zh * 4 + zz, c))

    def along_y(i, j):
        slot = y * 4 + mod(zl + j, 4)
        return remote(wg.at[slot], wg.at[slot], w_s.at[3 + 3 * j + i - 1], w_r.at[slot], dev(x, y + i, z, c))

    def arrival(slot):
        remote(wg.at[slot], wg.at[slot], w_s.at[0], w_r.at[slot], dev(x, y + 1, z, c)).wait_recv()

    for i in range(1, 4):
        out.start(along_z(i))
    for i in range(1, 4):
        out.start(along_y(i, 0))

    def peak(v, a, b):
        return jnp.max(jnp.max(jnp.abs(v[a:b]), axis=0, keepdims=True), axis=1, keepdims=True)

    m_top = [peak(momentum, a, b) for a, b in SLOT_ROWS]
    v_top = [peak(variance, a, b) for a, b in SLOT_ROWS]
    for i, slot in ((0, 0), (1, 4)):
        ex[i] = jnp.concatenate(
            [jnp.broadcast_to(m_top[slot], (4, 128)), jnp.broadcast_to(v_top[slot], (4, 128))], axis=0
        )
    owner = shard * 16 + rep

    def edge_copy(i):
        other = mod(owner + (1 if i else -1), 256)
        return remote(ex.at[i], fx.at[1 - i], e_s.at[i], e_r.at[1 - i], (other // 16, other % 16))

    for i in (0, 1):
        out.start(edge_copy(i))
    nm_ref[...] = fresh
    up_ref[...] = update

    for j in (1, 3, 2):
        arrival(y * 4 + mod(zl + j, 4))
        for i in range(1, 4):
            out.start(along_y(i, j))

    for i in (0, 1):
        edge_copy(i).wait_recv()
    flat = jnp.full((1, 128), owner, jnp.int32)
    for slot, i, live in ((0, 0, flat > 0), (4, 1, flat < 255)):
        m_top[slot] = jnp.where(live, jnp.maximum(m_top[slot], fx[i, 0:1]), m_top[slot])
        v_top[slot] = jnp.where(live, jnp.maximum(v_top[slot], fx[i, 4:5]), v_top[slot])
    lane = lax.broadcasted_iota(jnp.int32, (1, 128), 1)
    m_row = jnp.zeros((1, 128), F32)
    v_row = jnp.zeros((1, 128), F32)
    for i, (a, b) in enumerate(SLOT_ROWS):
        mn_ref[a:b, :] = momentum[a:b] / (m_top[i] + 1e-06)
        vn_ref[a:b, :] = variance[a:b] / (v_top[i] + 1e-06)
        m_row = jnp.where(lane == i, m_top[i], m_row)
        v_row = jnp.where(lane == i, v_top[i], v_row)
    tb_ref[0:1, :] = m_row
    tb_ref[1:2, :] = v_row

    for i in range(1, 4):
        for j in range(4):
            arrival(mod(y + i, 4) * 4 + j)
    for i in range(16):
        wt_ref[i * ROWS : (i + 1) * ROWS, :] = wg[i]
    out.finish()


def on_device(grads, momentum_codes, variance_codes, momentum_scale, variance_scale, master, step):
    block = jax.ShapeDtypeStruct((ROWS, 128), F32)
    vmem = pl.BlockSpec(memory_space=pltpu.VMEM)
    smem = pl.BlockSpec(memory_space=pltpu.SMEM)
    sem = pltpu.SemaphoreType.DMA

    def f32(*shape):
        return pltpu.VMEM(shape + (128,), F32)

    new_master, weights, update, m_norm, v_norm, table = pl.pallas_call(
        kernel,
        out_shape=(
            block,
            jax.ShapeDtypeStruct((16 * ROWS, 128), BF16),
            block,
            block,
            block,
            jax.ShapeDtypeStruct((2, 128), F32),
        ),
        in_specs=[pl.BlockSpec(memory_space=pl.ANY), vmem, vmem, smem, smem, vmem, smem],
        out_specs=(vmem,) * 6,
        scratch_shapes=[
            pltpu.VMEM((1, 1, HALF), BF16),
            pltpu.VMEM((1, 1, HALF), BF16),
            f32(4, 2, 16, RA),
            f32(4, 2, 16, RB),
            f32(8, 2, 8, RC),
            f32(6, 16, RA),
            f32(6, 16, RB),
            f32(14, 8, RC),
            f32(4, 2, 4, RA),
            f32(4, 2, 4, RB),
            f32(4, 4, RC),
            f32(6, 4, RA),
            f32(6, 4, RB),
            f32(8, RA),
            f32(8, RB),
            f32(7, RA),
            f32(7, RB),
            f32(15, RC),
            f32(1),
            f32(31, 1),
            f32(1),
            f32(7, 1),
            f32(2, 8),
            f32(2, 8),
            pltpu.VMEM((16, ROWS, 128), BF16),
            sem((32,)),
        ]
        + [sem((n,)) for n in (32, 6, 6, 14, 6, 6, 7, 7, 15, 31, 7, 2) for _ in range(2)]
        + [sem((15,)), sem((16,))],
        compiler_params=pltpu.CompilerParams(
            collective_id=0, has_side_effects=True, vmem_limit_bytes=48 * 2**20
        ),
        name="adamw_step",
    )(
        grads,
        momentum_codes.reshape(ROWS, 128),
        variance_codes.reshape(ROWS, 128),
        momentum_scale,
        variance_scale,
        master.reshape(ROWS, 128),
        step,
    )
    return (
        new_master.reshape(-1),
        weights.reshape(-1),
        update.reshape(-1),
        m_norm.reshape(-1),
        v_norm.reshape(-1),
        table[0, :5],
        table[1, :5],
    )


def solution(mesh):
    own = P(("shard", "rep"))
    return jax.shard_map(
        on_device,
        mesh=mesh,
        in_specs=(P("shard", "rep", None), own, own, own, own, own, P()),
        out_specs=(own, P("shard"), own, own, own, own, own),
        check_vma=False,
    )
```
